32 devices in a mesh: dp: 8 (over z, y), tensor: 4 (over x, core).
Axes of the slice: x: 2, y: 2, z: 4, core: 2. Of those that a mesh axis runs over, the one named last changes fastest.
Arguments:
- layer_in: bfloat16 [4096, 768], P(('dp', 'tensor')), may hold values from -6 to 6
- encoder_states: bfloat16 [4096, 768], P(('dp', 'tensor')), may hold values from -6 to 6
- grad_out: bfloat16 [4096, 768], P(('dp', 'tensor')), may hold values from -6 to 6
- buckets: int32 [8, 512, 512], P('dp'), may hold values from 0 to 31, as said below
- keep: int32 [8, 512, 512], P('dp'), may hold values from 0 to 1, as said below
- wq_self: bfloat16 [768, 768], P('dp', 'tensor'), may hold values from -0.02734375 to 0.02734375
- wk_self: bfloat16 [768, 768], P('dp', 'tensor'), may hold values from -0.21875 to 0.21875
- wv_self: bfloat16 [768, 768], P('dp', 'tensor'), may hold values from -0.21875 to 0.21875
- wo_self: bfloat16 [768, 768], P('tensor', 'dp'), may hold values from -0.875 to 0.875
- wq_cross: bfloat16 [768, 768], P('dp', 'tensor'), may hold values from -0.02734375 to 0.02734375
- wk_cross: bfloat16 [768, 768], P('dp', 'tensor'), may hold values from -0.21875 to 0.21875
- wv_cross: bfloat16 [768, 768], P('dp', 'tensor'), may hold values from -0.21875 to 0.21875
- wo_cross: bfloat16 [768, 768], P('tensor', 'dp'), may hold values from -0.875 to 0.875
- w_gate: bfloat16 [768, 2048], P('dp', 'tensor'), may hold values from -0.21875 to 0.21875
- w_up: bfloat16 [768, 2048], P('dp', 'tensor'), may hold values from -0.21875 to 0.21875
- w_down: bfloat16 [2048, 768], P('tensor', 'dp'), may hold values from -0.125 to 0.125
- norm_scales: bfloat16 [3, 768], P(None, 'dp'), may hold values from 0.5 to 1.5
- rel_bias: float32 [32, 12], P(None, 'tensor'), may hold values from -4 to 4
Outputs:
- layer_out: bfloat16 [4096, 768], P(('dp', 'tensor'))
- grad_in: float32 [4096, 768], P(('dp', 'tensor'))
- grad_encoder: float32 [4096, 768], P(('dp', 'tensor'))
- grad_wq_self: float32 [768, 768], P('dp', 'tensor')
- grad_wk_self: float32 [768, 768], P('dp', 'tensor')
- grad_wv_self: float32 [768, 768], P('dp', 'tensor')
- grad_wo_self: float32 [768, 768], P('tensor', 'dp')
- grad_wq_cross: float32 [768, 768], P('dp', 'tensor')
- grad_wk_cross: float32 [768, 768], P('dp', 'tensor')
- grad_wv_cross: float32 [768, 768], P('dp', 'tensor')
- grad_wo_cross: float32 [768, 768], P('tensor', 'dp')
- grad_w_gate: float32 [768, 2048], P('dp', 'tensor')
- grad_w_up: float32 [768, 2048], P('dp', 'tensor')
- grad_w_down: float32 [2048, 768], P('tensor', 'dp')
- grad_norm_scales: float32 [3, 768], P(None, ('dp', 'tensor'))
- grad_rel_bias: float32 [32, 12], P(None, 'tensor')
The draws below stay inside these ranges and needn't reach their ends.
Inputs may be any that keep to these rules, and one draw needn't show every extreme that they name: Each sequence holds one to three documents, the first of 256 positions or more. buckets[s, i, j] is the T5 bucket (exact below 16, logarithmic up to distance 128, the last bucket beyond) of i - j where keep = 1, and 0 elsewhere. keep[s, i, j] = 1 exactly where key j lies in the same document as query i and j <= i.
All inputs are finite; a program needn't handle non-finite values.
Results may differ from the reference program's by a relative error of at most 0.02.
Values may be sent and summed in bfloat16 or wider, within the bound.
A program may use at most 128 MiB of HBM per device.

```python
import math
import jax
import jax.numpy as jnp
import numpy as np
from jax import lax

D = 768
H = 12
DH = 64
FF = 2048
NBUCKET = 32
L = 512
HD = 768
SEQS = 8
TOKENS = 4096


def distance_table(length):
    exact_count = NBUCKET // 2
    bucket_table = np.zeros(length, dtype=np.int32)
    for distance in range(length):
        if distance < exact_count:
            bucket_table[distance] = distance
        else:
            spread = int(math.log(distance / exact_count) / math.log(128 / exact_count) * (NBUCKET - exact_count))
            bucket_table[distance] = min(exact_count + spread, NBUCKET - 1)
    return bucket_table


def doc_layout(key):
    base_key = jax.random.fold_in(key, 11)
    bucket_table = jnp.asarray(distance_table(L))

    def sequence_layout(number):
        cuts = jax.random.randint(jax.random.fold_in(base_key, number), (2,), L // 2, L + L // 4)
        places = lax.iota(jnp.int32, L)
        documents = (places >= cuts[0]).astype(jnp.int32) + (places >= cuts[1]).astype(jnp.int32)
        distance = places[:, None] - places[None, :]
        allowed = (documents[:, None] == documents[None, :]) & (distance >= 0)
        bucket_rows = jnp.where(allowed, bucket_table[jnp.clip(distance, 0, L - 1)], 0)
        return (bucket_rows.astype(jnp.int32), allowed.astype(jnp.int32))
    return lax.map(sequence_layout, lax.iota(jnp.int32, SEQS))


def draw_buckets(key, part):
    return doc_layout(key)[0]


def draw_keep(key, part):
    return doc_layout(key)[1]


def block_scale(key, dims, split, smallest, largest):
    loudness = 1.0
    for axis_at, shards_of in split:
        steps = jax.random.uniform(jax.random.fold_in(jax.random.fold_in(key, 6), axis_at), (shards_of,), jnp.float32, smallest / len(split), largest / len(split))
        loudness = loudness * jnp.repeat(jnp.exp(steps), dims[axis_at] // shards_of).reshape((-1,) + (1,) * (len(dims) - 1 - axis_at))
    return loudness


def centred(stream_key, extent, scale, reach, cuts=(), kind=jnp.bfloat16):
    entries = scale * jax.random.normal(stream_key, extent, jnp.float32)
    if cuts:
        entries = entries * block_scale(stream_key, extent, cuts, -0.22, 0.18)
    return jnp.clip(entries, -reach, reach).astype(kind)


def setup_inputs(seed: int = 0) -> dict:
    key_list = jax.random.split(jax.random.key(seed), 19)
    return {
        "layer_in": centred(key_list[0], (TOKENS, D), 1.0, 6.0, ((0, 32),)),
        "encoder_states": centred(key_list[1], (TOKENS, D), 1.0, 6.0, ((0, 32),)),
        "grad_out": centred(key_list[2], (TOKENS, D), 1.0, 6.0, ((0, 32),)),
        "buckets": draw_buckets(jax.random.fold_in(key_list[18], 71), 0),
        "keep": draw_keep(jax.random.fold_in(key_list[18], 71), 0),
        "wq_self": centred(key_list[5], (D, HD), (D * DH) ** -0.5, 0.02734375, ((0, 8), (1, 4))),
        "wk_self": centred(key_list[6], (D, HD), D ** -0.5, 0.21875, ((0, 8), (1, 4))),
        "wv_self": centred(key_list[7], (D, HD), D ** -0.5, 0.21875, ((0, 8), (1, 4))),
        "wo_self": centred(key_list[8], (HD, D), (HD // 16) ** -0.5, 0.875, ((0, 4), (1, 8))),
        "wq_cross": centred(key_list[9], (D, HD), (D * DH) ** -0.5, 0.02734375, ((0, 8), (1, 4))),
        "wk_cross": centred(key_list[10], (D, HD), D ** -0.5, 0.21875, ((0, 8), (1, 4))),
        "wv_cross": centred(key_list[11], (D, HD), D ** -0.5, 0.21875, ((0, 8), (1, 4))),
        "wo_cross": centred(key_list[12], (HD, D), (HD // 16) ** -0.5, 0.875, ((0, 4), (1, 8))),
        "w_gate": centred(key_list[13], (D, FF), D ** -0.5, 0.21875, ((0, 8), (1, 4))),
        "w_up": centred(key_list[14], (D, FF), D ** -0.5, 0.21875, ((0, 8), (1, 4))),
        "w_down": centred(key_list[15], (FF, D), FF ** -0.5, 0.125, ((0, 4), (1, 8))),
        "norm_scales": jnp.clip(1.0 + 0.1 * jax.random.normal(key_list[16], (3, D), jnp.float32), 0.5, 1.5).astype(jnp.bfloat16),
        "rel_bias": centred(key_list[17], (NBUCKET, H), 0.8, 4.0, ((1, 4),), jnp.float32),
    }


NORM_EPSILON = 1e-06
MASKED_SCORE = -1e+30
GELU_CUBIC = 0.044715

def to_half(values):
    return values.astype(jnp.bfloat16)

def matmul(left_side, right_side):
    return jnp.dot(left_side, right_side, preferred_element_type=jnp.float32)

def left_contract(left_side, right_side):
    return jnp.dot(left_side.T, right_side, preferred_element_type=jnp.float32)

def right_contract(left_side, right_side):
    return jnp.dot(left_side, right_side.T, preferred_element_type=jnp.float32)

def gelu_pair(values):
    root_scale = math.sqrt(2.0 / math.pi)
    interior = root_scale * (values + GELU_CUBIC * values * values * values)
    tangent = jnp.tanh(interior)
    activated = 0.5 * values * (1.0 + tangent)
    slope = 0.5 * (1.0 + tangent) + 0.5 * values * (1.0 - tangent * tangent) * root_scale * (1.0 + 3.0 * GELU_CUBIC * values * values)
    return (activated, slope)

def norm_forward(stream, gain):
    inverse = lax.rsqrt(lax.optimization_barrier(jnp.mean(stream * stream, axis=-1, keepdims=True)) + NORM_EPSILON)
    unit_rows = stream * inverse
    return (unit_rows, inverse, to_half(unit_rows * gain.astype(jnp.float32)))

def norm_backward(incoming, unit_rows, inverse, gain):
    scaled = incoming * gain.astype(jnp.float32)
    result = inverse * (scaled - unit_rows * lax.optimization_barrier(jnp.mean(scaled * unit_rows, axis=-1, keepdims=True)))
    return (result, lax.optimization_barrier(jnp.sum(incoming * unit_rows, axis=0)))

def head_split(matrix):
    return matrix.reshape(matrix.shape[0], -1, DH).astype(jnp.float32)

def score_matrix(queries, keys, bias, allowed):
    logits = jnp.einsum('qhd,khd->hqk', head_split(queries), head_split(keys))
    if bias is not None:
        logits = jnp.where(allowed[None], logits + bias, MASKED_SCORE)
    return logits

def attend(queries, keys, values, bias, allowed):
    logits = score_matrix(queries, keys, bias, allowed)
    row_max = lax.optimization_barrier(jnp.max(logits, axis=-1, keepdims=True))
    log_total = row_max + jnp.log(lax.optimization_barrier(jnp.sum(jnp.exp(logits - row_max), axis=-1, keepdims=True)))
    probs_half = lax.optimization_barrier(to_half(jnp.exp(logits - log_total))).astype(jnp.float32)
    mixed = jnp.einsum('hqk,khd->qhd', probs_half, head_split(values))
    return (to_half(mixed.reshape(queries.shape[0], -1)), log_total)

def attend_back(queries, keys, values, bias, allowed, log_total, grad_mixed):
    logits = score_matrix(queries, keys, bias, allowed)
    probs_full = jnp.exp(logits - log_total)
    probs_half = lax.optimization_barrier(to_half(probs_full)).astype(jnp.float32)
    grad_values = to_half(jnp.einsum('hqk,qhd->khd', probs_half, head_split(grad_mixed)).reshape(keys.shape[0], -1))
    grad_probs = jnp.einsum('qhd,khd->hqk', head_split(grad_mixed), head_split(values))
    centre = lax.optimization_barrier(jnp.sum(probs_full * grad_probs, axis=-1, keepdims=True))
    grad_logits = probs_full * (grad_probs - centre)
    logits_half = lax.optimization_barrier(to_half(grad_logits)).astype(jnp.float32)
    grad_queries = to_half(jnp.einsum('hqk,khd->qhd', logits_half, head_split(keys)).reshape(queries.shape[0], -1))
    grad_keys = to_half(jnp.einsum('hqk,qhd->khd', logits_half, head_split(queries)).reshape(keys.shape[0], -1))
    return (grad_queries, grad_keys, grad_values, grad_logits)

def one_sequence(stream_rows, source_rows, grad_rows, bucket_rows, keep_rows, params):
    wq_self, wk_self, wv_self, wo_self, wq_cross, wk_cross, wv_cross, wo_cross, w_gate, w_up, w_down, norm_scales, rel_bias = params
    allowed = keep_rows == 1
    bias_self = jnp.transpose(rel_bias[bucket_rows], (2, 0, 1))
    stream_in = stream_rows.astype(jnp.float32)
    unit_one, inverse_one, first_normed_input = norm_forward(stream_in, norm_scales[0])
    self_q = to_half(matmul(first_normed_input, wq_self))
    self_k = to_half(matmul(first_normed_input, wk_self))
    self_v = to_half(matmul(first_normed_input, wv_self))
    mixed_self, total_self = attend(self_q, self_k, self_v, bias_self, allowed)
    stream_one = stream_in + matmul(mixed_self, wo_self)
    unit_two, inverse_two, normed_two = norm_forward(stream_one, norm_scales[1])
    cross_q = to_half(matmul(normed_two, wq_cross))
    cross_k = to_half(matmul(source_rows, wk_cross))
    cross_v = to_half(matmul(source_rows, wv_cross))
    mixed_cross, total_cross = attend(cross_q, cross_k, cross_v, None, None)
    stream_two = stream_one + matmul(mixed_cross, wo_cross)
    unit_three, inverse_three, normed_three = norm_forward(stream_two, norm_scales[2])
    gate_rows = matmul(normed_three, w_gate)
    up_rows = matmul(normed_three, w_up)
    activated, slope = gelu_pair(gate_rows)
    hidden = to_half(activated * up_rows)
    layer_rows = to_half(stream_two + matmul(hidden, w_down))
    grad_hidden = right_contract(grad_rows, w_down)
    grad_w_down = left_contract(hidden, grad_rows)
    grad_gate = to_half(grad_hidden * up_rows * slope)
    grad_up = to_half(grad_hidden * activated)
    grad_w_gate = left_contract(normed_three, grad_gate)
    grad_w_up = left_contract(normed_three, grad_up)
    grad_normed_three = right_contract(grad_gate, w_gate) + right_contract(grad_up, w_up)
    back_three, gain_three = norm_backward(grad_normed_three, unit_three, inverse_three, norm_scales[2])
    grad_stream_two = grad_rows.astype(jnp.float32) + back_three
    grad_two_half = to_half(grad_stream_two)
    grad_mixed_cross = to_half(right_contract(grad_two_half, wo_cross))
    grad_wo_cross = left_contract(mixed_cross, grad_two_half)
    grad_q_cross, cross_key_gradient, grad_v_cross, unused_logits = attend_back(cross_q, cross_k, cross_v, None, None, total_cross, grad_mixed_cross)
    grad_wq_cross = left_contract(normed_two, grad_q_cross)
    grad_wk_cross = left_contract(source_rows, cross_key_gradient)
    grad_wv_cross = left_contract(source_rows, grad_v_cross)
    grad_source = right_contract(cross_key_gradient, wk_cross) + right_contract(grad_v_cross, wv_cross)
    back_two, gain_two = norm_backward(right_contract(grad_q_cross, wq_cross), unit_two, inverse_two, norm_scales[1])
    grad_stream_one = grad_stream_two + back_two
    grad_one_half = to_half(grad_stream_one)
    grad_mixed_self = to_half(right_contract(grad_one_half, wo_self))
    grad_wo_self = left_contract(mixed_self, grad_one_half)
    grad_q_self, grad_k_self, grad_v_self, grad_logits_self = attend_back(self_q, self_k, self_v, bias_self, allowed, total_self, grad_mixed_self)
    grad_bias = jax.ops.segment_sum(jnp.transpose(grad_logits_self, (1, 2, 0)).reshape(-1, grad_logits_self.shape[0]), bucket_rows.reshape(-1), num_segments=NBUCKET)
    grad_wq_self = left_contract(first_normed_input, grad_q_self)
    grad_wk_self = left_contract(first_normed_input, grad_k_self)
    grad_wv_self = left_contract(first_normed_input, grad_v_self)
    grad_normed_one = right_contract(grad_q_self, wq_self) + right_contract(grad_k_self, wk_self) + right_contract(grad_v_self, wv_self)
    back_one, gain_one = norm_backward(grad_normed_one, unit_one, inverse_one, norm_scales[0])
    grad_stream_in = grad_stream_one + back_one
    grads = (grad_wq_self, grad_wk_self, grad_wv_self, grad_wo_self, grad_wq_cross, grad_wk_cross, grad_wv_cross, grad_wo_cross, grad_w_gate, grad_w_up, grad_w_down, jnp.stack([gain_one, gain_two, gain_three]), grad_bias)
    return (layer_rows, grad_stream_in, grad_source, grads)

def add_pair(first, second):
    return first + second

def reference(layer_in, encoder_states, grad_out, buckets, keep, wq_self, wk_self, wv_self, wo_self, wq_cross, wk_cross, wv_cross, wo_cross, w_gate, w_up, w_down, norm_scales, rel_bias):
    params = (wq_self, wk_self, wv_self, wo_self, wq_cross, wk_cross, wv_cross, wo_cross, w_gate, w_up, w_down, norm_scales, rel_bias)
    zero_grads = tuple((jnp.zeros(param.shape, jnp.float32) for param in params))

    def step(summed_totals, pieces):
        layer_rows, grad_stream_in, grad_source, grads = one_sequence(pieces[0], pieces[1], pieces[2], pieces[3], pieces[4], params)
        return (jax.tree.map(add_pair, summed_totals, grads), (layer_rows, grad_stream_in, grad_source))
    sequences = (layer_in.reshape(SEQS, L, D), encoder_states.reshape(SEQS, L, D), grad_out.reshape(SEQS, L, D), buckets, keep)
    summed_totals, outputs = lax.scan(step, zero_grads, sequences)
    return (outputs[0].reshape(TOKENS, D), outputs[1].reshape(TOKENS, D), outputs[2].reshape(TOKENS, D), summed_totals[0], summed_totals[1], summed_totals[2], summed_totals[3], summed_totals[4], summed_totals[5], summed_totals[6], summed_totals[7], summed_totals[8], summed_totals[9], summed_totals[10], summed_totals[11], summed_totals[12])
```

```python
import math

import jax
import jax.numpy as jnp
import numpy as np
from jax import lax
from jax.experimental import pallas as pl
from jax.experimental.pallas import tpu as pltpu
from jax.sharding import PartitionSpec as P

DH = 64
NBUCKET = 32
L = 512
BLOCK = 128
NORM_EPSILON = 1e-06
MASKED_SCORE = -1e30
GELU_CUBIC = 0.044715
F32 = jnp.float32
BF16 = jnp.bfloat16


def to_half(values):
    return values.astype(BF16)


def matmul(left_side, right_side):
    return jnp.dot(left_side, right_side, preferred_element_type=F32)


def left_contract(left_side, right_side):
    return lax.dot_general(left_side, right_side, (((0,), (0,)), ((), ())), preferred_element_type=F32)


def right_contract(left_side, right_side):
    return lax.dot_general(left_side, right_side, (((1,), (1,)), ((), ())), preferred_element_type=F32)


def gelu_pair(values):
    root_scale = math.sqrt(2.0 / math.pi)
    interior = root_scale * (values + GELU_CUBIC * values * values * values)
    tangent = jnp.tanh(interior)
    activated = 0.5 * values * (1.0 + tangent)
    slope = 0.5 * (1.0 + tangent) + 0.5 * values * (1.0 - tangent * tangent) * root_scale * (
        1.0 + 3.0 * GELU_CUBIC * values * values
    )
    return (activated, slope)


def unit_norm(stream):
    inverse = lax.rsqrt(jnp.mean(stream * stream, axis=-1, keepdims=True) + NORM_EPSILON)
    return (stream * inverse, inverse)


def norm_backward(incoming, unit_rows, inverse, gain):
    scaled = incoming * gain
    result = inverse * (scaled - unit_rows * jnp.mean(scaled * unit_rows, axis=-1, keepdims=True))
    return (result, jnp.sum(incoming * unit_rows, axis=0))


def distance_indicator():
    exact = NBUCKET // 2
    distance = (-np.arange(L)) % L
    log_part = exact + np.floor(
        np.log(np.maximum(distance, 1) / exact) / np.log(128 / exact) * (NBUCKET - exact)
    ).astype(np.int64)
    bucket = np.where(distance < exact, distance, np.minimum(log_part, NBUCKET - 1))
    return (bucket[None, :] == np.arange(NBUCKET)[:, None]).astype(np.float32)


def whole(*shape_and_type):
    return jax.ShapeDtypeStruct(*shape_and_type)


MESH = pl.DeviceIdType.MESH
VMEM_LIMIT = 62 * 1024 * 1024
ROW_TILE = 16
LOTS = 2


def flipped(index, bits):
    step = 1
    while step <= bits:
        if bits & step:
            index = index + step - 2 * step * lax.rem(lax.div(index, step), 2)
        step *= 2
    return index


def subsets(bits):
    sums = [0]
    for bit in bits:
        sums += [bit | other for other in sums]
    return sums


def split_bits(size):
    return [1 << k for k in range(size.bit_length() - 1)]


class Links:
    def __init__(self, inner):
        self.dp = lax.axis_index("dp")
        self.place = lax.div(self.dp, inner)
        self.inner = inner
        self.me = lax.axis_index("tensor")
        self.partner = flipped(self.me, 1)
        self.across = flipped(self.me, 2)
        self.pending = []

    def send(self, source, target, send_sem, recv_sem, peer):
        copy = pltpu.make_async_remote_copy(
            src_ref=source,
            dst_ref=target,
            send_sem=send_sem,
            recv_sem=recv_sem,
            device_id=peer,
            device_id_type=MESH,
        )
        copy.start()
        self.pending.append(copy)
        return copy

    def along_dp(self, bit):
        return dict(dp=flipped(self.dp, bit * self.inner))

    def drain(self):
        for copy in self.pending:
            copy.wait_send()


class Gather:
    def __init__(self, links, buffer, sems, row, order):
        self.links, self.buffer = links, buffer
        self.send_sems, self.recv_sems, self.row = *sems, row
        self.order = order
        self.copies = {}
        self.next = 0

    def forward(self, relative, bits):
        owner = flipped(self.links.place, relative)
        for bit in bits:
            slot = relative | bit
            self.copies[slot] = self.links.send(
                self.buffer.at[owner],
                self.buffer.at[owner],
                self.send_sems.at[self.row, slot],
                self.recv_sems.at[self.row, slot],
                self.links.along_dp(bit),
            )

    def launch(self):
        self.forward(0, self.order)

    def step(self):
        bit = self.order[self.next]
        for relative in subsets(self.order[:self.next]):
            self.copies[relative | bit].wait_recv()
            self.forward(relative | bit, self.order[self.next + 1:])
        self.next += 1

    def finish(self):
        while self.next < len(self.order):
            self.step()


class Reduce:
    def __init__(self, links, parts, landed, sems, row, order):
        self.links, self.parts, self.landed = links, parts, landed
        self.send_sems, self.recv_sems, self.row = *sems, row
        self.order = order
        self.copies = {}
        self.next = 0

    def total(self, relative, bits):
        value = self.parts[flipped(self.links.place, relative)].astype(F32)
        for bit in bits:
            self.copies[relative | bit].wait_recv()
            value = value + self.landed[relative | bit].astype(F32)
        return value

    def step(self):
        bit = self.order[self.next]
        for later in subsets(self.order[self.next + 1:]):
            relative = later | bit
            owner = flipped(self.links.place, relative)
            if self.next:
                self.parts[owner] = to_half(self.total(relative, self.order[:self.next]))
            self.copies[relative] = self.links.send(
                self.parts.at[owner],
                self.landed.at[relative],
                self.send_sems.at[self.row, relative],
                self.recv_sems.at[self.row, relative],
                self.links.along_dp(bit),
            )
        self.next += 1

    def finish(self):
        while self.next < len(self.order):
            self.step()
        return self.total(0, self.order)


class Spread:
    def __init__(self, links, held, sems, row, lots):
        self.links, self.held, self.row = links, held, row
        self.send_sems, self.recv_sems = sems
        self.share = held.shape[0] // 4
        self.lot_rows = self.share // lots
        self.over, self.near, self.ahead = {}, {}, {}

    def rows(self, index, lot):
        start = index * self.share + lot * self.lot_rows
        return pl.ds(pl.multiple_of(start, self.lot_rows), self.lot_rows)

    def send(self, index, lot, sem, peer):
        block = self.held.at[self.rows(index, lot)]
        return self.links.send(
            block,
            block,
            self.send_sems.at[self.row, 3 * lot + sem],
            self.recv_sems.at[self.row, 3 * lot + sem],
            dict(tensor=peer),
        )

    def launch(self, values, lot=0):
        links = self.links
        self.held[self.rows(links.me, lot), :] = values
        self.over[lot] = self.send(links.me, lot, 0, links.across)
        self.near[lot] = self.send(links.me, lot, 1, links.partner)

    def middle(self, lot=0):
        self.over[lot].wait_recv()
        self.ahead[lot] = self.send(self.links.across, lot, 2, self.links.partner)

    def finish(self, lot=0):
        self.near[lot].wait_recv()
        self.ahead[lot].wait_recv()


class Collect:
    def __init__(self, links, part, sent, landed, sems, row):
        self.links, self.part, self.sent, self.landed = links, part, sent, landed
        self.send_sems, self.recv_sems = sems
        self.row = row
        self.lot_rows = sent.shape[2] // LOTS
        self.over = {}

    def send(self, index, sem, rows, peer):
        return self.links.send(
            self.sent.at[self.row, index, rows],
            self.landed.at[self.row, index, rows],
            self.send_sems.at[self.row, sem],
            self.recv_sems.at[self.row, sem],
            dict(tensor=peer),
        )

    def lot(self, lot):
        return slice(lot * self.lot_rows, (lot + 1) * self.lot_rows)

    def launch(self):
        links, row = self.links, self.row
        every = pl.ds(0, self.sent.shape[2])
        self.sent[row, 0] = to_half(self.part(flipped(links.me, 3)))
        self.far = self.send(0, 0, every, links.partner)
        self.mine_far = self.part(links.across)
        self.sent[row, 1] = to_half(self.part(links.partner))
        self.near = self.send(1, 1, every, links.partner)

    def middle(self):
        self.far.wait_recv()
        for lot in range(LOTS):
            rows = self.lot(lot)
            self.sent[self.row, 2, rows] = to_half(
                self.mine_far[rows] + self.landed[self.row, 0, rows].astype(F32)
            )
            block = pl.ds(lot * self.lot_rows, self.lot_rows)
            self.over[lot] = self.send(2, 2 + lot, block, self.links.across)
        self.mine = self.part(self.links.me)
        self.near.wait_recv()
        self.mine = self.mine + self.landed[self.row, 1].astype(F32)

    def finish(self, lot):
        self.over[lot].wait_recv()
        rows = self.lot(lot)
        return self.mine[rows] + self.landed[self.row, 2, rows].astype(F32)


def flat(buffer, low=0, high=None):
    value = buffer[...] if high is None else buffer[:, :, low:high]
    return value.reshape(-1, value.shape[-1])


def attend_block(q, k, v, bias, allowed):
    logits = right_contract(q, k)
    if bias is not None:
        logits = jnp.where(allowed, logits + bias, MASKED_SCORE)
    row_max = jnp.max(logits, axis=-1, keepdims=True)
    powers = jnp.exp(logits - row_max)
    probs = to_half(powers / jnp.sum(powers, axis=-1, keepdims=True))
    return probs, to_half(matmul(probs, v))


def attend(qkv_ref, base_ref, keep_ref, mixed_ref, probs_ref, between):
    masked = base_ref is not None
    width = mixed_ref.shape[1]
    heads = width // DH
    for block in range(L // BLOCK):
        rows = slice(block * BLOCK, (block + 1) * BLOCK)
        reach = (block + 1) * BLOCK if masked else L
        allowed = keep_ref[0, rows, :reach] == 1 if masked else None
        pieces = []
        for h in range(heads):
            bias = None
            if masked:
                base = base_ref[h]
                tiles = [
                    pltpu.roll(base, 8 * t, 1) if t else base
                    for t in range(block * BLOCK // 8, (block + 1) * BLOCK // 8)
                ]
                bias = jnp.concatenate(tiles, axis=0)[:, :reach]
            probs, mixed = attend_block(
                qkv_ref[rows, h * DH:(h + 1) * DH],
                qkv_ref[:reach, width + h * DH:width + (h + 1) * DH],
                qkv_ref[:reach, 2 * width + h * DH:2 * width + (h + 1) * DH],
                bias,
                allowed,
            )
            probs_ref[h, rows, :reach] = probs
            pieces.append(mixed)
        mixed_ref[rows, :] = jnp.concatenate(pieces, axis=1)
        if block < len(between) and between[block] is not None:
            between[block]()


def attend_back(masked, qkv_ref, probs_ref, gm_ref, grad_ref, key_total, value_total, between):
    width = gm_ref.shape[1]
    heads = width // DH
    totals = []
    turn = 0
    for h in range(heads):
        cq = slice(h * DH, (h + 1) * DH)
        ck = slice(width + h * DH, width + (h + 1) * DH)
        cv = slice(2 * width + h * DH, 2 * width + (h + 1) * DH)
        diag = jnp.zeros((8, L), F32)
        for block in reversed(range(L // BLOCK)):
            rows = slice(block * BLOCK, (block + 1) * BLOCK)
            reach = (block + 1) * BLOCK if masked else L
            probs = probs_ref[h, rows, :reach]
            gm = gm_ref[rows, cq]
            grad_probs = right_contract(gm, qkv_ref[:reach, cv])
            probs_full = probs.astype(F32)
            centre = jnp.sum(probs_full * grad_probs, axis=-1, keepdims=True)
            grad_logits = probs_full * (grad_probs - centre)
            half = to_half(grad_logits)
            grad_ref[rows, cq] = to_half(matmul(half, qkv_ref[:reach, ck]))
            key_part = left_contract(half, qkv_ref[rows, cq])
            value_part = left_contract(probs, gm)
            if block == L // BLOCK - 1:
                key_total[:, :] = key_part
                value_total[:, :] = value_part
            else:
                key_total[:reach, :] += key_part
                value_total[:reach, :] += value_part
            if masked:
                for t in range(BLOCK // 8):
                    tile = grad_logits[8 * t:8 * t + 8]
                    if reach < L:
                        tile = jnp.concatenate([tile, jnp.zeros((8, L - reach), F32)], axis=1)
                    shift = (L - (block * BLOCK + 8 * t)) % L
                    diag = diag + (pltpu.roll(tile, shift, 1) if shift else tile)
            if turn < len(between) and between[turn] is not None:
                between[turn]()
            turn += 1
        grad_ref[:, ck] = to_half(key_total[...])
        grad_ref[:, cv] = to_half(value_total[...])
        if masked:
            total = diag[0:1]
            for s in range(1, 8):
                total = total + pltpu.roll(diag[s:s + 1], L - s, 1)
            totals.append(total)
    return totals


class Names:
    def __init__(self, names, refs):
        for name, ref in zip(names, refs, strict=True):
            setattr(self, name, ref)


def layer_kernel(names, inner, *refs):
    r = Names(names, refs)
    links = Links(inner)
    W = r.wq_s.shape[1]
    F = r.w_gate.shape[1]
    D = r.layer_in.shape[1]
    share = r.layer_in.shape[0]
    heads = W // DH
    dp_bits = split_bits(lax.axis_size("dp"))

    barrier = pltpu.get_barrier_semaphore()
    peers = [dict(dp=flipped(links.dp, bit)) for bit in dp_bits]
    peers += [dict(tensor=links.partner), dict(tensor=links.across)]
    for peer in peers:
        pl.semaphore_signal(barrier, inc=1, device_id=peer, device_id_type=MESH)
    pl.semaphore_wait(barrier, len(peers))

    bits = split_bits(r.w_qk_s.shape[0])
    far_first, near_first = bits[::-1], bits[:1] + bits[:0:-1]
    numbers = dict(gather=0, reduce=0, spread=0, collect=0)

    def number(kind):
        numbers[kind] += 1
        return numbers[kind] - 1

    def gather(buffer, order=far_first):
        return Gather(links, buffer, (r.gather_send, r.gather_recv), number("gather"), order)

    def reduce(parts, landed, order=far_first[::-1]):
        return Reduce(links, parts, landed, (r.reduce_send, r.reduce_recv), number("reduce"), order)

    def spread(held, lots=1):
        return Spread(links, held, (r.spread_send, r.spread_recv), number("spread"), lots)

    def collect(part):
        return Collect(links, part, r.sent, r.landed, (r.collect_send, r.collect_recv), number("collect"))

    def block_of(ref, block):
        return ref[pl.ds(pl.multiple_of(block * share, share), share), :]

    def stage(buffer, *parts):
        buffer[links.place] = jnp.concatenate(parts, axis=1)

    def turned(ref):
        return to_half(jnp.transpose(ref[...].astype(F32)))

    def put(group, product):
        group.parts[...] = to_half(product).reshape(group.parts.shape)
        group.step()

    def steps(*groups):
        for group in groups:
            group.step()

    qk_s, vo_s, kv_c, qo_c = gather(r.w_qk_s), gather(r.w_vo_s), gather(r.w_kv_c), gather(r.w_qo_c)
    gate_up, down_t, gains = gather(r.w_gate_up), gather(r.w_down_t, near_first), gather(r.gains_all)
    g_dn = reduce(r.p_dn, r.l_dn, near_first[::-1])
    g_gate, g_up = reduce(r.p_gate, r.l_gate), reduce(r.p_up, r.l_up)
    g_kv_c, g_qo_c = reduce(r.p_kv_c, r.l_kv_c), reduce(r.p_qo_c, r.l_qo_c)
    g_wo_s, g_qk_s = reduce(r.p_wo_s, r.l_wo_s), reduce(r.p_qk_s, r.l_qk_s)
    g_v_s = reduce(r.p_v_s, r.l_v_s, near_first[::-1])

    layer_rows = spread(r.stream_all)
    stage(r.w_qk_s, r.wq_s[...], r.wk_s[...])
    qk_s.launch()
    layer_rows.launch(r.layer_in[...])
    own_scales = r.scales[...].astype(F32)
    own_scales = jnp.concatenate([own_scales, jnp.zeros((3, 128 - own_scales.shape[1]), F32)], axis=1)
    r.gains_all[links.place] = jnp.concatenate([own_scales, jnp.zeros((5, 128), F32)], axis=0)
    gains.launch()
    stage(r.w_vo_s, r.wv_s[...], turned(r.wo_s))
    vo_s.launch()
    stage(r.w_kv_c, r.wk_c[...], r.wv_c[...])
    stage(r.w_qo_c, r.wq_c[...], turned(r.wo_c))
    stage(r.w_gate_up, r.w_gate[...], r.w_up[...])
    r.w_down_t[links.place] = r.w_down[...]
    bias_columns = jnp.transpose(r.rel_bias[...])
    for h in range(heads):
        row = jnp.sum(r.indicator[...] * bias_columns[:, h:h + 1], axis=0, keepdims=True)
        r.base[h] = jnp.concatenate([pltpu.roll(row, s, 1) if s else row for s in range(8)], axis=0)

    steps(qk_s, gains)
    steps(qk_s, vo_s, gains)
    kv_c.launch()
    layer_rows.middle()
    vo_s.step()
    source_rows = spread(r.source_all)
    source_rows.launch(r.source[...])
    layer_rows.finish()
    gains.finish()
    width = r.scales.shape[1]
    gain = jnp.concatenate([r.gains_all[o][:, :width] for o in range(r.gains_all.shape[0])], axis=1)
    gain_one, gain_two, gain_three = gain[0:1], gain[1:2], gain[2:3]
    for block in range(L // BLOCK):
        rows = slice(block * BLOCK, (block + 1) * BLOCK)
        unit = unit_norm(r.stream_all[rows, :].astype(F32))[0]
        r.unit_one[rows, :] = unit
        r.rows_one[rows, :] = to_half(unit * gain_one)
    kv_c.step()
    qo_c.launch()
    qk_s.finish()
    r.qkv_s[:, :2 * W] = to_half(matmul(r.rows_one[...], flat(r.w_qk_s)))
    kv_c.step()
    vo_s.finish()
    r.qkv_s[:, 2 * W:] = to_half(matmul(r.rows_one[...], flat(r.w_vo_s, 0, W)))
    qo_c.step()
    gate_up.launch()
    source_rows.middle()
    grad_rows = spread(r.grad_all)

    def after_one():
        source_rows.finish()
        grad_rows.launch(r.grad_out[...])

    attend(r.qkv_s, r.base, r.keep, r.mixed_s, r.probs_s, (after_one, None, qo_c.step))

    one = collect(lambda b: right_contract(block_of(r.mixed_s, b), flat(r.w_vo_s, W, 2 * W)))
    one.launch()
    one.middle()
    kv_c.finish()
    r.qkv_c[:, W:] = to_half(matmul(r.source_all[...], flat(r.w_kv_c)))
    gate_up.step()
    down_t.launch()
    rows_two = spread(r.rows_two, LOTS)
    for lot in range(LOTS):
        rows = one.lot(lot)
        stream_one = r.layer_in[rows, :].astype(F32) + one.finish(lot)
        r.stream_one[rows, :] = stream_one
        rows_two.launch(to_half(unit_norm(stream_one)[0] * gain_two), lot)
    grad_rows.middle()
    qo_c.finish()
    gate_up.step()
    for lot in range(LOTS):
        rows_two.middle(lot)
    grad_rows.finish()
    for lot in range(LOTS):
        rows_two.finish(lot)
    r.qkv_c[:, :W] = to_half(matmul(r.rows_two[...], flat(r.w_qo_c, 0, W)))

    attend(r.qkv_c, None, None, r.mixed_c, r.probs_c, (None, down_t.step, None))

    two = collect(lambda b: right_contract(block_of(r.mixed_c, b), flat(r.w_qo_c, W, 2 * W)))
    two.launch()
    two.middle()
    down_t.step()
    rows_three = spread(r.rows_three, LOTS)
    for lot in range(LOTS):
        rows = two.lot(lot)
        stream_two = r.stream_one[rows, :] + two.finish(lot)
        r.stream_two[rows, :] = stream_two
        rows_three.launch(to_half(unit_norm(stream_two)[0] * gain_three), lot)
    down_t.finish()
    r.grad_hidden[...] = matmul(r.grad_all[...], flat(r.w_down_t))
    for lot in range(LOTS):
        rows_three.middle(lot)
    gate_up.finish()
    for lot in range(LOTS):
        rows_three.finish(lot)

    half_width = F // 2
    for piece in range(2):
        columns = slice(piece * half_width, (piece + 1) * half_width)
        shifted = slice(F + piece * half_width, F + (piece + 1) * half_width)
        gate_w = flat(r.w_gate_up, columns.start, columns.stop)
        up_w = flat(r.w_gate_up, shifted.start, shifted.stop)
        for lot in range(2):
            rows = slice(lot * L // 2, (lot + 1) * L // 2)
            up_part = matmul(r.rows_three[rows, :], up_w)
            activated, slope = gelu_pair(matmul(r.rows_three[rows, :], gate_w))
            grad_part = r.grad_hidden[rows, columns]
            r.hidden[rows, columns] = to_half(activated * up_part)
            r.grad_gate_up[rows, columns] = to_half(grad_part * up_part * slope)
            r.grad_gate_up[rows, shifted] = to_half(grad_part * activated)

    three = collect(lambda b: right_contract(block_of(r.grad_gate_up, b), flat(r.w_gate_up)))
    three.launch()
    three.middle()
    put(g_gate, left_contract(r.rows_three[...], r.grad_gate_up[:, :F]))
    put(g_dn, left_contract(r.grad_all[...], r.hidden[...]))
    two_half = spread(r.grad_two, LOTS)
    gain_grad_three = 0.0
    for lot in range(LOTS):
        rows = three.lot(lot)
        unit, inverse = unit_norm(r.stream_two[rows, :])
        back, gain_part = norm_backward(three.finish(lot), unit, inverse, gain_three)
        gain_grad_three = gain_grad_three + gain_part
        grad_stream_two = r.grad_out[rows, :].astype(F32) + back
        r.grad_stream_two[rows, :] = grad_stream_two
        two_half.launch(to_half(grad_stream_two), lot)
    put(g_up, left_contract(r.rows_three[...], r.grad_gate_up[:, F:]))
    for lot in range(LOTS):
        two_half.middle(lot)
    for lot in range(LOTS):
        two_half.finish(lot)

    late_out = collect(lambda b: right_contract(block_of(r.hidden, b), flat(r.w_down_t)))
    r.gm[...] = to_half(matmul(r.grad_two[...], flat(r.w_qo_c, W, 2 * W)))
    late_out.launch()
    late_out.middle()

    def finish_out():
        for lot in range(LOTS):
            rows = late_out.lot(lot)
            r.layer_out[rows, :] = to_half(r.stream_two[rows, :] + late_out.finish(lot))

    attend_back(
        False, r.qkv_c, r.probs_c, r.gm, r.grad_c, r.key_total, r.value_total,
        (None, None, None, None, None, None, None, g_gate.step, None, g_dn.step, finish_out),
    )

    four = collect(lambda b: right_contract(block_of(r.grad_c, b)[:, :W], flat(r.w_qo_c, 0, W)))
    four.launch()
    four.middle()
    put(g_kv_c, left_contract(r.source_all[...], r.grad_c[:, W:]))
    steps(g_up, g_gate, g_dn)
    one_half = spread(r.grad_one, LOTS)
    gain_grad_two = 0.0
    for lot in range(LOTS):
        rows = four.lot(lot)
        unit, inverse = unit_norm(r.stream_one[rows, :])
        back, gain_part = norm_backward(four.finish(lot), unit, inverse, gain_two)
        gain_grad_two = gain_grad_two + gain_part
        grad_stream_one = r.grad_stream_two[rows, :] + back
        r.grad_stream_one[rows, :] = grad_stream_one
        one_half.launch(to_half(grad_stream_one), lot)
    put(
        g_qo_c,
        jnp.concatenate(
            [
                left_contract(r.rows_two[...], r.grad_c[:, :W]),
                left_contract(r.grad_two[...], r.mixed_c[...]),
            ],
            axis=1,
        ),
    )
    g_up.step()
    for lot in range(LOTS):
        one_half.middle(lot)
    for lot in range(LOTS):
        one_half.finish(lot)

    late_source = collect(lambda b: right_contract(block_of(r.grad_c, b)[:, W:], flat(r.w_kv_c)))
    r.gm[...] = to_half(matmul(r.grad_one[...], flat(r.w_vo_s, W, 2 * W)))
    late_source.launch()
    late_source.middle()
    put(g_wo_s, left_contract(r.grad_one[...], r.mixed_s[...]))

    def finish_source():
        for lot in range(LOTS):
            r.grad_source[late_source.lot(lot), :] = late_source.finish(lot)

    diagonals = attend_back(
        True, r.qkv_s, r.probs_s, r.gm, r.grad_s, r.key_total, r.value_total,
        (None, None, g_kv_c.step, None, None, None, None, finish_source, None, g_qo_c.step, g_kv_c.step),
    )

    put(g_qk_s, left_contract(r.rows_one[...], r.grad_s[:, :2 * W]))
    put(g_v_s, left_contract(r.rows_one[...], r.grad_s[:, 2 * W:]))
    gain_parts = []

    def last_part(b):
        rows = block_of(r.grad_s, b)
        part = right_contract(rows[:, :2 * W], flat(r.w_qk_s)) + right_contract(
            rows[:, 2 * W:], flat(r.w_vo_s, 0, W)
        )
        gain_parts.append(jnp.sum(part * block_of(r.unit_one, b), axis=0))
        return part

    five = collect(last_part)
    five.launch()
    five.middle()
    gain_grad_one = gain_parts[0] + gain_parts[1] + gain_parts[2] + gain_parts[3]
    fill = jnp.zeros((1, D - L), F32)
    lines = [g.reshape(1, D) for g in (gain_grad_one, gain_grad_two, gain_grad_three)]
    lines += [jnp.concatenate([d, fill], axis=1) for d in diagonals]
    lines.append(jnp.zeros((8 - len(lines), D), F32))
    r.small_sum[0] = jnp.concatenate(lines, axis=0)
    small_copies = []

    def small_start():
        at = len(small_copies)
        small_copies.append(
            links.send(
                r.small_sum.at[at], r.small_landed.at[at], r.small_send.at[at], r.small_recv.at[at], peers[at]
            )
        )

    def small_end():
        at = len(small_copies)
        small_copies[-1].wait_recv()
        r.small_sum[at] = r.small_sum[at - 1] + r.small_landed[at - 1]
        if at == len(peers) - 2:
            r.small_out[0] = r.small_sum[at]
        if at < len(peers):
            small_start()

    small_start()
    steps(g_wo_s, g_qo_c)
    small_end()
    r.o_gate[...] = g_gate.finish()
    r.o_dn[...] = g_dn.finish()
    for lot in range(LOTS):
        rows = five.lot(lot)
        unit, inverse = unit_norm(r.layer_in[rows, :].astype(F32))
        back, unused = norm_backward(five.finish(lot), unit, inverse, gain_one)
        r.grad_in[rows, :] = r.grad_stream_one[rows, :] + back
    small_end()
    r.o_up[...] = g_up.finish()
    r.o_kv_c[...] = g_kv_c.finish()
    g_v_s.step()
    g_wo_s.step()
    small_end()
    g_qk_s.step()
    r.o_qo_c[...] = g_qo_c.finish()
    g_v_s.step()
    small_end()
    r.o_wo_s[...] = g_wo_s.finish()
    g_qk_s.step()
    while len(small_copies) < len(peers):
        small_end()
    small_end()
    r.small_out[1] = r.small_sum[len(peers)]
    r.o_v_s[...] = g_v_s.finish()
    r.o_qk_s[...] = g_qk_s.finish()
    links.drain()


def run_layer(inner, operands):
    W = operands["wq_s"].shape[1]
    F = operands["w_gate"].shape[1]
    rows, D = operands["layer_in"].shape
    share = operands["wq_s"].shape[0]
    n = D // share
    heads = W // DH
    steps = len(split_bits(lax.axis_size("dp"))) + 2
    widths = dict(dn=F, gate=F, up=F, kv_c=2 * W, qo_c=2 * W, wo_s=W, qk_s=2 * W, v_s=W)
    outs = dict(layer_out=whole((rows, D), BF16), grad_in=whole((rows, D), F32), grad_source=whole((rows, D), F32))
    for name, columns in widths.items():
        outs["o_" + name] = whole((share, columns), F32)
    outs.update(small_out=whole((2, 8, D), F32))

    def vmem(*shape, kind=BF16):
        return pltpu.VMEM(shape, kind)

    def sems(name, *shape):
        scratch[name + "_send"] = pltpu.SemaphoreType.DMA(shape)
        scratch[name + "_recv"] = pltpu.SemaphoreType.DMA(shape)

    tokens, heads_part, stream = vmem(L, D), vmem(L, W), vmem(rows, D, kind=F32)
    triple, pairs, total = vmem(L, 3 * W), vmem(heads, L, L), vmem(L, DH, kind=F32)
    weights = vmem(n, share, 2 * W)
    scratch = dict(
        w_qk_s=weights,
        w_vo_s=weights,
        w_kv_c=weights,
        w_qo_c=weights,
        w_gate_up=vmem(n, share, 2 * F),
        w_down_t=vmem(n, share, F),
        gains_all=vmem(n, 8, 128, kind=F32),
        base=vmem(heads, 8, L, kind=F32),
        unit_one=vmem(L, D, kind=F32),
        stream_all=tokens,
        source_all=tokens,
        grad_all=tokens,
        rows_one=tokens,
        rows_two=tokens,
        rows_three=tokens,
        grad_two=tokens,
        grad_one=tokens,
        qkv_s=triple,
        qkv_c=triple,
        grad_s=triple,
        grad_c=triple,
        probs_s=pairs,
        probs_c=pairs,
        mixed_s=heads_part,
        mixed_c=heads_part,
        gm=heads_part,
        hidden=vmem(L, F),
        grad_gate_up=vmem(L, 2 * F),
        grad_hidden=vmem(L, F, kind=F32),
        key_total=total,
        value_total=total,
        stream_one=stream,
        stream_two=stream,
        grad_stream_two=stream,
        grad_stream_one=stream,
        sent=vmem(7, 3, rows, D),
        landed=vmem(7, 3, rows, D),
        small_sum=vmem(steps + 1, 8, D, kind=F32),
        small_landed=vmem(steps, 8, D, kind=F32),
    )
    for name, columns in widths.items():
        scratch["p_" + name] = vmem(n, share, columns)
        scratch["l_" + name] = vmem(n, share, columns)
    sems("gather", 7, n)
    sems("reduce", len(widths), n)
    sems("spread", 7, 3 * LOTS)
    sems("collect", 7, 2 + LOTS)
    sems("small", steps)
    names = list(operands) + list(outs) + list(scratch)
    results = pl.pallas_call(
        lambda *refs: layer_kernel(names, inner, *refs),
        out_shape=tuple(outs.values()),
        in_specs=[pl.BlockSpec(memory_space=pltpu.VMEM)] * len(operands),
        out_specs=tuple(pl.BlockSpec(memory_space=pltpu.VMEM) for _ in outs),
        scratch_shapes=list(scratch.values()),
        name="layer",
        compiler_params=pltpu.CompilerParams(
            collective_id=1, has_side_effects=True, vmem_limit_bytes=VMEM_LIMIT
        ),
    )(*operands.values())
    return dict(zip(outs, results, strict=True))


def write_kernel(names, *refs):
    r = Names(names, refs)
    W = r.o_wo_s.shape[1]
    D = r.layer_out.shape[1]
    own = r.grad_scales.shape[1]
    r.layer[...] = r.layer_out[...]
    r.back[...] = r.grad_in[...]
    r.encoder[...] = r.grad_source[...]
    r.wq_s[...] = r.o_qk_s[:, :W]
    r.wk_s[...] = r.o_qk_s[:, W:]
    r.wv_s[...] = r.o_v_s[...]
    r.wo_s[...] = jnp.transpose(r.o_wo_s[...])
    r.wq_c[...] = r.o_qo_c[:, :W]
    r.wk_c[...] = r.o_kv_c[:, :W]
    r.wv_c[...] = r.o_kv_c[:, W:]
    r.wo_c[...] = jnp.transpose(r.o_qo_c[:, W:])
    r.w_gate[...] = r.o_gate[...]
    r.w_up[...] = r.o_up[...]
    r.w_down[...] = r.o_dn[...]
    place = lax.axis_index("dp") * lax.axis_size("tensor") + lax.axis_index("tensor")
    turn = lax.rem(D - place * own, D)
    r.grad_scales[...] = pltpu.roll(r.small_out[1], turn, 1)[:3, :own]
    sums = jnp.concatenate(
        [
            jnp.sum(r.indicator[...] * r.small_out[0][3 + h:4 + h, :L], axis=1, keepdims=True)
            for h in range(W // DH)
        ],
        axis=1,
    )
    r.grad_bias[...] = jnp.transpose(sums)


def write_out(sums, indicator):
    rows, D = sums["layer_out"].shape
    share, W = sums["o_wo_s"].shape
    F = sums["o_dn"].shape[1]
    devices = lax.axis_size("dp") * lax.axis_size("tensor")
    square = whole((share, W), F32)
    turned = whole((W, share), F32)
    wide = whole((share, F), F32)
    outs = dict(
        layer=whole((rows, D), BF16),
        back=whole((rows, D), F32),
        encoder=whole((rows, D), F32),
        wq_s=square,
        wk_s=square,
        wv_s=square,
        wo_s=turned,
        wq_c=square,
        wk_c=square,
        wv_c=square,
        wo_c=turned,
        w_gate=wide,
        w_up=wide,
        w_down=wide,
        grad_scales=whole((3, D // devices), F32),
        grad_bias=whole((W // DH, NBUCKET), F32),
    )
    operands = dict(sums, indicator=indicator)
    names = list(operands) + list(outs)
    results = pl.pallas_call(
        lambda *refs: write_kernel(names, *refs),
        out_shape=tuple(outs.values()),
        in_specs=[pl.BlockSpec(memory_space=pltpu.VMEM)] * len(operands),
        out_specs=tuple(pl.BlockSpec(memory_space=pltpu.VMEM) for _ in outs),
        name="write_out",
        compiler_params=pltpu.CompilerParams(vmem_limit_bytes=VMEM_LIMIT),
    )(*operands.values())
    final = dict(zip(outs, results, strict=True))
    final.update(w_down=final["w_down"].T, grad_bias=final["grad_bias"].T)
    return tuple(final.values())


def per_device(
    layer_in,
    encoder_states,
    grad_out,
    buckets,
    keep,
    wq_self,
    wk_self,
    wv_self,
    wo_self,
    wq_cross,
    wk_cross,
    wv_cross,
    wo_cross,
    w_gate,
    w_up,
    w_down,
    norm_scales,
    rel_bias,
):
    size = lax.axis_size("dp")
    inner = 1
    while (wq_self.shape[0] * inner) % (2 * ROW_TILE) and inner < size:
        inner *= 2
    groups = [list(range(start, start + inner)) for start in range(0, size, inner)]

    def joined(weights, axis):
        if inner == 1:
            return weights
        return lax.all_gather(weights, "dp", axis=axis, tiled=True, axis_index_groups=groups)

    indicator = jnp.asarray(distance_indicator())
    operands = dict(
        layer_in=layer_in,
        source=encoder_states,
        grad_out=grad_out,
        keep=keep,
        wq_s=joined(wq_self, 0),
        wk_s=joined(wk_self, 0),
        wv_s=joined(wv_self, 0),
        wo_s=joined(wo_self, 1),
        wq_c=joined(wq_cross, 0),
        wk_c=joined(wk_cross, 0),
        wv_c=joined(wv_cross, 0),
        wo_c=joined(wo_cross, 1),
        w_gate=joined(w_gate, 0),
        w_up=joined(w_up, 0),
        w_down=joined(w_down, 1).T,
        scales=joined(norm_scales, 1),
        rel_bias=rel_bias.T,
        indicator=indicator,
    )
    sums = run_layer(inner, operands)
    if inner > 1:
        for name in [name for name in sums if name.startswith("o_")]:
            sums[name] = lax.psum_scatter(
                sums[name], "dp", scatter_dimension=0, tiled=True, axis_index_groups=groups
            )
    return write_out(sums, indicator)


def solution(mesh):
    in_specs = (
        P(("dp", "tensor"), None),
        P(("dp", "tensor"), None),
        P(("dp", "tensor"), None),
        P("dp", None, None),
        P("dp", None, None),
        P("dp", "tensor"),
        P("dp", "tensor"),
        P("dp", "tensor"),
        P("tensor", "dp"),
        P("dp", "tensor"),
        P("dp", "tensor"),
        P("dp", "tensor"),
        P("tensor", "dp"),
        P("dp", "tensor"),
        P("dp", "tensor"),
        P("tensor", "dp"),
        P(None, "dp"),
        P(None, "tensor"),
    )
    out_specs = (
        P(("dp", "tensor"), None),
        P(("dp", "tensor"), None),
        P(("dp", "tensor"), None),
        P("dp", "tensor"),
        P("dp", "tensor"),
        P("dp", "tensor"),
        P("tensor", "dp"),
        P("dp", "tensor"),
        P("dp", "tensor"),
        P("dp", "tensor"),
        P("tensor", "dp"),
        P("dp", "tensor"),
        P("dp", "tensor"),
        P("tensor", "dp"),
        P(None, ("dp", "tensor")),
        P(None, "tensor"),
    )
    return jax.shard_map(
        per_device, mesh=mesh, in_specs=in_specs, out_specs=out_specs, check_vma=False
    )
```

```python
import math

import jax
import jax.numpy as jnp
import numpy as np
from jax import lax
from jax.experimental import pallas as pl
from jax.experimental.pallas import tpu as pltpu
from jax.sharding import PartitionSpec as P

DH = 64
NBUCKET = 32
L = 512
BLOCK = 128
NORM_EPSILON = 1e-06
MASKED_SCORE = -1e30
GELU_CUBIC = 0.044715
F32 = jnp.float32
BF16 = jnp.bfloat16


def to_half(values):
    return values.astype(BF16)


def matmul(left_side, right_side):
    return jnp.dot(left_side, right_side, preferred_element_type=F32)


def left_contract(left_side, right_side):
    return lax.dot_general(left_side, right_side, (((0,), (0,)), ((), ())), preferred_element_type=F32)


def right_contract(left_side, right_side):
    return lax.dot_general(left_side, right_side, (((1,), (1,)), ((), ())), preferred_element_type=F32)


def gelu_pair(values):
    root_scale = math.sqrt(2.0 / math.pi)
    interior = root_scale * (values + GELU_CUBIC * values * values * values)
    tangent = jnp.tanh(interior)
    activated = 0.5 * values * (1.0 + tangent)
    slope = 0.5 * (1.0 + tangent) + 0.5 * values * (1.0 - tangent * tangent) * root_scale * (
        1.0 + 3.0 * GELU_CUBIC * values * values
    )
    return (activated, slope)


def unit_norm(stream):
    inverse = lax.rsqrt(jnp.mean(stream * stream, axis=-1, keepdims=True) + NORM_EPSILON)
    return (stream * inverse, inverse)


def norm_backward(incoming, unit_rows, inverse, gain):
    scaled = incoming * gain
    result = inverse * (scaled - unit_rows * jnp.mean(scaled * unit_rows, axis=-1, keepdims=True))
    return (result, jnp.sum(incoming * unit_rows, axis=0))


def distance_indicator():
    exact = NBUCKET // 2
    distance = (-np.arange(L)) % L
    log_part = exact + np.floor(
        np.log(np.maximum(distance, 1) / exact) / np.log(128 / exact) * (NBUCKET - exact)
    ).astype(np.int64)
    bucket = np.where(distance < exact, distance, np.minimum(log_part, NBUCKET - 1))
    return (bucket[None, :] == np.arange(NBUCKET)[:, None]).astype(np.float32)


def whole(*shape_and_type):
    return jax.ShapeDtypeStruct(*shape_and_type)


MESH = pl.DeviceIdType.MESH
VMEM_LIMIT = 62 * 1024 * 1024
ROW_TILE = 16
LOTS = 2


def flipped(index, bits):
    step = 1
    while step <= bits:
        if bits & step:
            index = index + step - 2 * step * lax.rem(lax.div(index, step), 2)
        step *= 2
    return index


def subsets(bits):
    sums = [0]
    for bit in bits:
        sums += [bit | other for other in sums]
    return sums


def split_bits(size):
    return [1 << k for k in range(size.bit_length() - 1)]


class Links:
    def __init__(self, inner):
        self.dp = lax.axis_index("dp")
        self.place = lax.div(self.dp, inner)
        self.inner = inner
        self.me = lax.axis_index("tensor")
        self.partner = flipped(self.me, 1)
        self.across = flipped(self.me, 2)
        self.pending = []

    def send(self, source, target, send_sem, recv_sem, peer):
        copy = pltpu.make_async_remote_copy(
            src_ref=source,
            dst_ref=target,
            send_sem=send_sem,
            recv_sem=recv_sem,
            device_id=peer,
            device_id_type=MESH,
        )
        copy.start()
        self.pending.append(copy)
        return copy

    def along_dp(self, bit):
        return dict(dp=flipped(self.dp, bit * self.inner))

    def drain(self):
        for copy in self.pending:
            copy.wait_send()


class Gather:
    def __init__(self, links, buffer, sems, row, order):
        self.links, self.buffer = links, buffer
        self.send_sems, self.recv_sems, self.row = *sems, row
        self.order = order
        self.copies = {}
        self.next = 0

    def forward(self, relative, bits):
        owner = flipped(self.links.place, relative)
        for bit in bits:
            slot = relative | bit
            self.copies[slot] = self.links.send(
                self.buffer.at[owner],
                self.buffer.at[owner],
                self.send_sems.at[self.row, slot],
                self.recv_sems.at[self.row, slot],
                self.links.along_dp(bit),
            )

    def launch(self):
        self.forward(0, self.order)

    def step(self):
        bit = self.order[self.next]
        for relative in subsets(self.order[:self.next]):
            self.copies[relative | bit].wait_recv()
            self.forward(relative | bit, self.order[self.next + 1:])
        self.next += 1

    def finish(self):
        while self.next < len(self.order):
            self.step()


class Reduce:
    def __init__(self, links, parts, landed, sems, row, order):
        self.links, self.parts, self.landed = links, parts, landed
        self.send_sems, self.recv_sems, self.row = *sems, row
        self.order = order
        self.copies = {}
        self.next = 0

    def total(self, relative, bits):
        value = self.parts[flipped(self.links.place, relative)].astype(F32)
        for bit in bits:
            self.copies[relative | bit].wait_recv()
            value = value + self.landed[relative | bit].astype(F32)
        return value

    def step(self):
        bit = self.order[self.next]
        for later in subsets(self.order[self.next + 1:]):
            relative = later | bit
            owner = flipped(self.links.place, relative)
            if self.next:
                self.parts[owner] = to_half(self.total(relative, self.order[:self.next]))
            self.copies[relative] = self.links.send(
                self.parts.at[owner],
                self.landed.at[relative],
                self.send_sems.at[self.row, relative],
                self.recv_sems.at[self.row, relative],
                self.links.along_dp(bit),
            )
        self.next += 1

    def finish(self):
        while self.next < len(self.order):
            self.step()
        return self.total(0, self.order)


class Spread:
    def __init__(self, links, held, sems, row, lots):
        self.links, self.held, self.row = links, held, row
        self.send_sems, self.recv_sems = sems
        self.share = held.shape[0] // 4
        self.lot_rows = self.share // lots
        self.over, self.near, self.ahead = {}, {}, {}

    def rows(self, index, lot):
        start = index * self.share + lot * self.lot_rows
        return pl.ds(pl.multiple_of(start, self.lot_rows), self.lot_rows)

    def send(self, index, lot, sem, peer):
        block = self.held.at[self.rows(index, lot)]
        return self.links.send(
            block,
            block,
            self.send_sems.at[self.row, 3 * lot + sem],
            self.recv_sems.at[self.row, 3 * lot + sem],
            dict(tensor=peer),
        )

    def launch(self, values, lot=0):
        links = self.links
        self.held[self.rows(links.me, lot), :] = values
        self.over[lot] = self.send(links.me, lot, 0, links.across)
        self.near[lot] = self.send(links.me, lot, 1, links.partner)

    def middle(self, lot=0):
        self.over[lot].wait_recv()
        self.ahead[lot] = self.send(self.links.across, lot, 2, self.links.partner)

    def finish(self, lot=0):
        self.near[lot].wait_recv()
        self.ahead[lot].wait_recv()


class Collect:
    def __init__(self, links, part, sent, landed, sems, row):
        self.links, self.part, self.sent, self.landed = links, part, sent, landed
        self.send_sems, self.recv_sems = sems
        self.row = row
        self.lot_rows = sent.shape[2] // LOTS
        self.over = {}

    def send(self, index, sem, rows, peer):
        return self.links.send(
            self.sent.at[self.row, index, rows],
            self.landed.at[self.row, index, rows],
            self.send_sems.at[self.row, sem],
            self.recv_sems.at[self.row, sem],
            dict(tensor=peer),
        )

    def lot(self, lot):
        return slice(lot * self.lot_rows, (lot + 1) * self.lot_rows)

    def launch(self):
        links, row = self.links, self.row
        every = pl.ds(0, self.sent.shape[2])
        self.sent[row, 0] = to_half(self.part(flipped(links.me, 3)))
        self.far = self.send(0, 0, every, links.partner)
        self.mine_far = self.part(links.across)
        self.sent[row, 1] = to_half(self.part(links.partner))
        self.near = self.send(1, 1, every, links.partner)

    def middle(self):
        self.far.wait_recv()
        for lot in range(LOTS):
            rows = self.lot(lot)
            self.sent[self.row, 2, rows] = to_half(
                self.mine_far[rows] + self.landed[self.row, 0, rows].astype(F32)
            )
            block = pl.ds(lot * self.lot_rows, self.lot_rows)
            self.over[lot] = self.send(2, 2 + lot, block, self.links.across)
        self.mine = self.part(self.links.me)
        self.near.wait_recv()
        self.mine = self.mine + self.landed[self.row, 1].astype(F32)

    def finish(self, lot):
        self.over[lot].wait_recv()
        rows = self.lot(lot)
        return self.mine[rows] + self.landed[self.row, 2, rows].astype(F32)


def flat(buffer, low=0, high=None):
    value = buffer[...] if high is None else buffer[:, :, low:high]
    return value.reshape(-1, value.shape[-1])


def attend_block(q, k, v, bias, allowed):
    logits = right_contract(q, k)
    if bias is not None:
        logits = jnp.where(allowed, logits + bias, MASKED_SCORE)
    row_max = jnp.max(logits, axis=-1, keepdims=True)
    powers = jnp.exp(logits - row_max)
    probs = to_half(powers / jnp.sum(powers, axis=-1, keepdims=True))
    return probs, to_half(matmul(probs, v))


def attend(qkv_ref, base_ref, keep_ref, mixed_ref, probs_ref, between):
    masked = base_ref is not None
    width = mixed_ref.shape[1]
    heads = width // DH
    for block in range(L // BLOCK):
        rows = slice(block * BLOCK, (block + 1) * BLOCK)
        reach = (block + 1) * BLOCK if masked else L
        allowed = keep_ref[0, rows, :reach] == 1 if masked else None
        pieces = []
        for h in range(heads):
            bias = None
            if masked:
                base = base_ref[h]
                tiles = [
                    pltpu.roll(base, 8 * t, 1) if t else base
                    for t in range(block * BLOCK // 8, (block + 1) * BLOCK // 8)
                ]
                bias = jnp.concatenate(tiles, axis=0)[:, :reach]
            probs, mixed = attend_block(
                qkv_ref[rows, h * DH:(h + 1) * DH],
                qkv_ref[:reach, width + h * DH:width + (h + 1) * DH],
                qkv_ref[:reach, 2 * width + h * DH:2 * width + (h + 1) * DH],
                bias,
                allowed,
            )
            probs_ref[h, rows, :reach] = probs
            pieces.append(mixed)
        mixed_ref[rows, :] = jnp.concatenate(pieces, axis=1)
        if block < len(between) and between[block] is not None:
            between[block]()


def attend_back(masked, qkv_ref, probs_ref, gm_ref, grad_ref, key_total, value_total, between):
    width = gm_ref.shape[1]
    heads = width // DH
    totals = []
    turn = 0
    for h in range(heads):
        cq = slice(h * DH, (h + 1) * DH)
        ck = slice(width + h * DH, width + (h + 1) * DH)
        cv = slice(2 * width + h * DH, 2 * width + (h + 1) * DH)
        diag = jnp.zeros((8, L), F32)
        for block in reversed(range(L // BLOCK)):
            rows = slice(block * BLOCK, (block + 1) * BLOCK)
            reach = (block + 1) * BLOCK if masked else L
            probs = probs_ref[h, rows, :reach]
            gm = gm_ref[rows, cq]
            grad_probs = right_contract(gm, qkv_ref[:reach, cv])
            probs_full = probs.astype(F32)
            centre = jnp.sum(probs_full * grad_probs, axis=-1, keepdims=True)
            grad_logits = probs_full * (grad_probs - centre)
            half = to_half(grad_logits)
            grad_ref[rows, cq] = to_half(matmul(half, qkv_ref[:reach, ck]))
            key_part = left_contract(half, qkv_ref[rows, cq])
            value_part = left_contract(probs, gm)
            if block == L // BLOCK - 1:
                key_total[:, :] = key_part
                value_total[:, :] = value_part
            else:
                key_total[:reach, :] += key_part
                value_total[:reach, :] += value_part
            if masked:
                for t in range(BLOCK // 8):
                    tile = grad_logits[8 * t:8 * t + 8]
                    if reach < L:
                        tile = jnp.concatenate([tile, jnp.zeros((8, L - reach), F32)], axis=1)
                    shift = (L - (block * BLOCK + 8 * t)) % L
                    diag = diag + (pltpu.roll(tile, shift, 1) if shift else tile)
            if turn < len(between) and between[turn] is not None:
                between[turn]()
            turn += 1
        grad_ref[:, ck] = to_half(key_total[...])
        grad_ref[:, cv] = to_half(value_total[...])
        if masked:
            total = diag[0:1]
            for s in range(1, 8):
                total = total + pltpu.roll(diag[s:s + 1], L - s, 1)
            totals.append(total)
    return totals


class Names:
    def __init__(self, names, refs):
        for name, ref in zip(names, refs, strict=True):
            setattr(self, name, ref)


def layer_kernel(names, inner, *refs):
    r = Names(names, refs)
    links = Links(inner)
    W = r.wq_s.shape[1]
    F = r.w_gate.shape[1]
    D = r.layer_in.shape[1]
    share = r.layer_in.shape[0]
    heads = W // DH
    dp_bits = split_bits(lax.axis_size("dp"))

    barrier = pltpu.get_barrier_semaphore()
    peers = [dict(dp=flipped(links.dp, bit)) for bit in dp_bits]
    peers += [dict(tensor=links.partner), dict(tensor=links.across)]
    for peer in peers:
        pl.semaphore_signal(barrier, inc=1, device_id=peer, device_id_type=MESH)
    pl.semaphore_wait(barrier, len(peers))

    bits = split_bits(r.w_qk_s.shape[0])
    far_first, near_first = bits[::-1], bits[:1] + bits[:0:-1]
    numbers = dict(gather=0, reduce=0, spread=0, collect=0)

    def number(kind):
        numbers[kind] += 1
        return numbers[kind] - 1

    def gather(buffer, order=far_first):
        return Gather(links, buffer, (r.gather_send, r.gather_recv), number("gather"), order)

    def reduce(parts, landed, order=far_first[::-1]):
        return Reduce(links, parts, landed, (r.reduce_send, r.reduce_recv), number("reduce"), order)

    def spread(held, lots=1):
        return Spread(links, held, (r.spread_send, r.spread_recv), number("spread"), lots)

    def collect(part):
        return Collect(links, part, r.sent, r.landed, (r.collect_send, r.collect_recv), number("collect"))

    def block_of(ref, block):
        return ref[pl.ds(pl.multiple_of(block * share, share), share), :]

    def stage(buffer, *parts):
        buffer[links.place] = jnp.concatenate(parts, axis=1)

    def turned(ref):
        return to_half(jnp.transpose(ref[...].astype(F32)))

    def put(group, product):
        group.parts[...] = to_half(product).reshape(group.parts.shape)
        group.step()

    def halves(product):
        product = to_half(product).reshape(-1, r.wq_s.shape[0], product.shape[1])
        middle = product.shape[1] // 2
        return product[:, :middle], product[:, middle:]

    def put_packed(group, product):
        group.parts[...] = jnp.concatenate(halves(product), axis=2)
        group.step()

    def unpack(target, total):
        middle, columns = total.shape[0], total.shape[1] // 2
        target[:middle, :] = total[:, :columns]
        target[middle:, :] = total[:, columns:]

    def steps(*groups):
        for group in groups:
            group.step()

    qk_s, vo_s, kv_c, qo_c = gather(r.w_qk_s), gather(r.w_vo_s), gather(r.w_kv_c), gather(r.w_qo_c)
    gate_up, down_t, gains = gather(r.w_gate_up), gather(r.w_down_t, near_first), gather(r.gains_all)
    g_dn = reduce(r.p_dn, r.l_dn, near_first[::-1])
    g_gate, g_up = reduce(r.p_gate, r.l_gate), reduce(r.p_up, r.l_up)
    g_kv_c, g_qo_c = reduce(r.p_kv_c, r.l_kv_c), reduce(r.p_qo_c, r.l_qo_c)
    g_wo_s, g_qa_s, g_qb_s = reduce(r.p_wo_s, r.l_wo_s), reduce(r.p_qa_s, r.l_qa_s), reduce(r.p_qb_s, r.l_qb_s)
    g_v_s = reduce(r.p_v_s, r.l_v_s, near_first[::-1])

    layer_rows = spread(r.stream_all)
    stage(r.w_qk_s, r.wq_s[...], r.wk_s[...])
    qk_s.launch()
    layer_rows.launch(r.layer_in[...])
    own_scales = r.scales[...].astype(F32)
    own_scales = jnp.concatenate([own_scales, jnp.zeros((3, 128 - own_scales.shape[1]), F32)], axis=1)
    r.gains_all[links.place] = jnp.concatenate([own_scales, jnp.zeros((5, 128), F32)], axis=0)
    gains.launch()
    stage(r.w_vo_s, r.wv_s[...], turned(r.wo_s))
    stage(r.w_kv_c, r.wk_c[...], r.wv_c[...])
    stage(r.w_qo_c, r.wq_c[...], turned(r.wo_c))
    stage(r.w_gate_up, r.w_gate[...], r.w_up[...])
    r.w_down_t[links.place] = r.w_down[...]
    bias_columns = jnp.transpose(r.rel_bias[...])
    for h in range(heads):
        row = jnp.sum(r.indicator[...] * bias_columns[:, h:h + 1], axis=0, keepdims=True)
        r.base[h] = jnp.concatenate([pltpu.roll(row, s, 1) if s else row for s in range(8)], axis=0)

    steps(qk_s, gains)
    vo_s.launch()
    steps(qk_s, gains)
    layer_rows.middle()
    vo_s.step()
    kv_c.launch()
    vo_s.step()
    source_rows = spread(r.source_all)
    source_rows.launch(r.source[...])
    layer_rows.finish()
    gains.finish()
    width = r.scales.shape[1]
    gain = jnp.concatenate([r.gains_all[o][:, :width] for o in range(r.gains_all.shape[0])], axis=1)
    gain_one, gain_two, gain_three = gain[0:1], gain[1:2], gain[2:3]
    for block in range(L // BLOCK):
        rows = slice(block * BLOCK, (block + 1) * BLOCK)
        unit = unit_norm(r.stream_all[rows, :].astype(F32))[0]
        r.unit_one[rows, :] = unit
        r.rows_one[rows, :] = to_half(unit * gain_one)
    kv_c.step()
    qo_c.launch()
    qk_s.finish()
    r.qkv_s[:, :2 * W] = to_half(matmul(r.rows_one[...], flat(r.w_qk_s)))
    kv_c.step()
    vo_s.finish()
    r.qkv_s[:, 2 * W:] = to_half(matmul(r.rows_one[...], flat(r.w_vo_s, 0, W)))
    qo_c.step()
    gate_up.launch()
    source_rows.middle()
    grad_rows = spread(r.grad_all)

    def after_one():
        source_rows.finish()
        grad_rows.launch(r.grad_out[...])

    attend(r.qkv_s, r.base, r.keep, r.mixed_s, r.probs_s, (after_one, None, qo_c.step))

    one = collect(lambda b: right_contract(block_of(r.mixed_s, b), flat(r.w_vo_s, W, 2 * W)))
    one.launch()
    one.middle()
    kv_c.finish()
    r.qkv_c[:, W:] = to_half(matmul(r.source_all[...], flat(r.w_kv_c)))
    gate_up.step()
    down_t.launch()
    rows_two = spread(r.rows_two, LOTS)
    for lot in range(LOTS):
        rows = one.lot(lot)
        stream_one = r.layer_in[rows, :].astype(F32) + one.finish(lot)
        r.stream_one[rows, :] = stream_one
        rows_two.launch(to_half(unit_norm(stream_one)[0] * gain_two), lot)
    grad_rows.middle()
    qo_c.finish()
    gate_up.step()
    for lot in range(LOTS):
        rows_two.middle(lot)
    grad_rows.finish()
    for lot in range(LOTS):
        rows_two.finish(lot)
    r.qkv_c[:, :W] = to_half(matmul(r.rows_two[...], flat(r.w_qo_c, 0, W)))

    attend(r.qkv_c, None, None, r.mixed_c, r.probs_c, (None, down_t.step, None))

    two = collect(lambda b: right_contract(block_of(r.mixed_c, b), flat(r.w_qo_c, W, 2 * W)))
    two.launch()
    two.middle()
    down_t.step()
    rows_three = spread(r.rows_three, LOTS)
    for lot in range(LOTS):
        rows = two.lot(lot)
        stream_two = r.stream_one[rows, :] + two.finish(lot)
        r.stream_two[rows, :] = stream_two
        rows_three.launch(to_half(unit_norm(stream_two)[0] * gain_three), lot)
    down_t.finish()
    r.grad_hidden[...] = matmul(r.grad_all[...], flat(r.w_down_t))
    for lot in range(LOTS):
        rows_three.middle(lot)
    gate_up.finish()
    for lot in range(LOTS):
        rows_three.finish(lot)

    half_width = F // 2
    for piece in range(2):
        columns = slice(piece * half_width, (piece + 1) * half_width)
        shifted = slice(F + piece * half_width, F + (piece + 1) * half_width)
        gate_w = flat(r.w_gate_up, columns.start, columns.stop)
        up_w = flat(r.w_gate_up, shifted.start, shifted.stop)
        for lot in range(2):
            rows = slice(lot * L // 2, (lot + 1) * L // 2)
            up_part = matmul(r.rows_three[rows, :], up_w)
            activated, slope = gelu_pair(matmul(r.rows_three[rows, :], gate_w))
            grad_part = r.grad_hidden[rows, columns]
            r.hidden[rows, columns] = to_half(activated * up_part)
            r.grad_gate_up[rows, columns] = to_half(grad_part * up_part * slope)
            r.grad_gate_up[rows, shifted] = to_half(grad_part * activated)

    three = collect(lambda b: right_contract(block_of(r.grad_gate_up, b), flat(r.w_gate_up)))
    three.launch()
    three.middle()
    put(g_gate, left_contract(r.rows_three[...], r.grad_gate_up[:, :F]))
    put(g_dn, left_contract(r.grad_all[...], r.hidden[...]))
    two_half = spread(r.grad_two, LOTS)
    gain_grad_three = 0.0
    for lot in range(LOTS):
        rows = three.lot(lot)
        unit, inverse = unit_norm(r.stream_two[rows, :])
        back, gain_part = norm_backward(three.finish(lot), unit, inverse, gain_three)
        gain_grad_three = gain_grad_three + gain_part
        grad_stream_two = r.grad_out[rows, :].astype(F32) + back
        r.grad_stream_two[rows, :] = grad_stream_two
        two_half.launch(to_half(grad_stream_two), lot)
    put(g_up, left_contract(r.rows_three[...], r.grad_gate_up[:, F:]))
    for lot in range(LOTS):
        two_half.middle(lot)
    for lot in range(LOTS):
        two_half.finish(lot)

    late_out = collect(lambda b: right_contract(block_of(r.hidden, b), flat(r.w_down_t)))
    r.gm[...] = to_half(matmul(r.grad_two[...], flat(r.w_qo_c, W, 2 * W)))
    late_out.launch()
    late_out.middle()

    def finish_out():
        for lot in range(LOTS):
            rows = late_out.lot(lot)
            r.layer_out[rows, :] = to_half(r.stream_two[rows, :] + late_out.finish(lot))

    attend_back(
        False, r.qkv_c, r.probs_c, r.gm, r.grad_c, r.key_total, r.value_total,
        (None, None, None, None, None, None, None, g_gate.step, None, g_dn.step, finish_out),
    )

    four = collect(lambda b: right_contract(block_of(r.grad_c, b)[:, :W], flat(r.w_qo_c, 0, W)))
    four.launch()
    four.middle()
    put(g_kv_c, left_contract(r.source_all[...], r.grad_c[:, W:]))
    steps(g_up, g_gate, g_dn)
    one_half = spread(r.grad_one, LOTS)
    gain_grad_two = 0.0
    for lot in range(LOTS):
        rows = four.lot(lot)
        unit, inverse = unit_norm(r.stream_one[rows, :])
        back, gain_part = norm_backward(four.finish(lot), unit, inverse, gain_two)
        gain_grad_two = gain_grad_two + gain_part
        grad_stream_one = r.grad_stream_two[rows, :] + back
        r.grad_stream_one[rows, :] = grad_stream_one
        one_half.launch(to_half(grad_stream_one), lot)
    put(
        g_qo_c,
        jnp.concatenate(
            [
                left_contract(r.rows_two[...], r.grad_c[:, :W]),
                left_contract(r.grad_two[...], r.mixed_c[...]),
            ],
            axis=1,
        ),
    )
    g_up.step()
    for lot in range(LOTS):
        one_half.middle(lot)
    for lot in range(LOTS):
        one_half.finish(lot)

    late_source = collect(lambda b: right_contract(block_of(r.grad_c, b)[:, W:], flat(r.w_kv_c)))
    r.gm[...] = to_half(matmul(r.grad_one[...], flat(r.w_vo_s, W, 2 * W)))
    late_source.launch()
    late_source.middle()
    put_packed(g_wo_s, left_contract(r.grad_one[...], r.mixed_s[...]))

    def finish_source():
        for lot in range(LOTS):
            r.grad_source[late_source.lot(lot), :] = late_source.finish(lot)

    diagonals = attend_back(
        True, r.qkv_s, r.probs_s, r.gm, r.grad_s, r.key_total, r.value_total,
        (None, None, g_kv_c.step, None, None, None, None, finish_source, None, g_qo_c.step, g_kv_c.step),
    )

    g_qa_s.parts[...], g_qb_s.parts[...] = halves(left_contract(r.rows_one[...], r.grad_s[:, :2 * W]))
    steps(g_qa_s, g_qb_s)
    put_packed(g_v_s, left_contract(r.rows_one[...], r.grad_s[:, 2 * W:]))
    gain_parts = []

    def last_part(b):
        rows = block_of(r.grad_s, b)
        part = right_contract(rows[:, :2 * W], flat(r.w_qk_s)) + right_contract(
            rows[:, 2 * W:], flat(r.w_vo_s, 0, W)
        )
        gain_parts.append(jnp.sum(part * block_of(r.unit_one, b), axis=0))
        return part

    five = collect(last_part)
    five.launch()
    five.middle()
    gain_grad_one = gain_parts[0] + gain_parts[1] + gain_parts[2] + gain_parts[3]
    fill = jnp.zeros((1, D - L), F32)
    lines = [g.reshape(1, D) for g in (gain_grad_one, gain_grad_two, gain_grad_three)]
    lines += [jnp.concatenate([d, fill], axis=1) for d in diagonals]
    lines.append(jnp.zeros((8 - len(lines), D), F32))
    r.small_sum[0] = jnp.concatenate(lines, axis=0)
    small_copies = []

    def small_start():
        at = len(small_copies)
        small_copies.append(
            links.send(
                r.small_sum.at[at], r.small_landed.at[at], r.small_send.at[at], r.small_recv.at[at], peers[at]
            )
        )

    def small_end():
        at = len(small_copies)
        small_copies[-1].wait_recv()
        r.small_sum[at] = r.small_sum[at - 1] + r.small_landed[at - 1]
        if at == len(peers) - 2:
            r.small_out[0] = r.small_sum[at]
        if at < len(peers):
            small_start()

    small_start()
    steps(g_wo_s, g_qo_c)
    r.o_gate[...] = g_gate.finish()
    r.o_dn[...] = g_dn.finish()
    steps(g_qa_s, g_v_s)
    small_end()
    for lot in range(LOTS):
        rows = five.lot(lot)
        unit, inverse = unit_norm(r.layer_in[rows, :].astype(F32))
        back, unused = norm_backward(five.finish(lot), unit, inverse, gain_one)
        r.grad_in[rows, :] = r.grad_stream_one[rows, :] + back
    r.o_up[...] = g_up.finish()
    r.o_kv_c[...] = g_kv_c.finish()
    small_end()
    steps(g_qb_s, g_qa_s, g_wo_s)
    small_end()
    r.o_qo_c[...] = g_qo_c.finish()
    g_v_s.step()
    g_qb_s.step()
    small_end()
    unpack(r.o_wo_s, g_wo_s.finish())
    middle = g_qa_s.parts.shape[1]
    r.o_qk_s[:middle, :] = g_qa_s.finish()
    while len(small_copies) < len(peers):
        small_end()
    small_end()
    r.small_out[1] = r.small_sum[len(peers)]
    unpack(r.o_v_s, g_v_s.finish())
    r.o_qk_s[middle:, :] = g_qb_s.finish()
    links.drain()


def run_layer(inner, operands):
    W = operands["wq_s"].shape[1]
    F = operands["w_gate"].shape[1]
    rows, D = operands["layer_in"].shape
    share = operands["wq_s"].shape[0]
    n = D // share
    heads = W // DH
    steps = len(split_bits(lax.axis_size("dp"))) + 2
    widths = dict(dn=F, gate=F, up=F, kv_c=2 * W, qo_c=2 * W, wo_s=W, qk_s=2 * W, v_s=W)
    outs = dict(layer_out=whole((rows, D), BF16), grad_in=whole((rows, D), F32), grad_source=whole((rows, D), F32))
    for name, columns in widths.items():
        outs["o_" + name] = whole((share, columns), F32)
    outs.update(small_out=whole((2, 8, D), F32))

    def vmem(*shape, kind=BF16):
        return pltpu.VMEM(shape, kind)

    def sems(name, *shape):
        scratch[name + "_send"] = pltpu.SemaphoreType.DMA(shape)
        scratch[name + "_recv"] = pltpu.SemaphoreType.DMA(shape)

    tokens, heads_part, stream = vmem(L, D), vmem(L, W), vmem(rows, D, kind=F32)
    triple, pairs, total = vmem(L, 3 * W), vmem(heads, L, L), vmem(L, DH, kind=F32)
    weights = vmem(n, share, 2 * W)
    scratch = dict(
        w_qk_s=weights,
        w_vo_s=weights,
        w_kv_c=weights,
        w_qo_c=weights,
        w_gate_up=vmem(n, share, 2 * F),
        w_down_t=vmem(n, share, F),
        gains_all=vmem(n, 8, 128, kind=F32),
        base=vmem(heads, 8, L, kind=F32),
        unit_one=vmem(L, D, kind=F32),
        stream_all=tokens,
        source_all=tokens,
        grad_all=tokens,
        rows_one=tokens,
        rows_two=tokens,
        rows_three=tokens,
        grad_two=tokens,
        grad_one=tokens,
        qkv_s=triple,
        qkv_c=triple,
        grad_s=triple,
        grad_c=triple,
        probs_s=pairs,
        probs_c=pairs,
        mixed_s=heads_part,
        mixed_c=heads_part,
        gm=heads_part,
        hidden=vmem(L, F),
        grad_gate_up=vmem(L, 2 * F),
        grad_hidden=vmem(L, F, kind=F32),
        key_total=total,
        value_total=total,
        stream_one=stream,
        stream_two=stream,
        grad_stream_two=stream,
        grad_stream_one=stream,
        sent=vmem(7, 3, rows, D),
        landed=vmem(7, 3, rows, D),
        small_sum=vmem(steps + 1, 8, D, kind=F32),
        small_landed=vmem(steps, 8, D, kind=F32),
    )
    whole_rows, half_rows = dict(dn=F, gate=F, up=F, kv_c=2 * W, qo_c=2 * W), dict(wo_s=2 * W, qa_s=2 * W, qb_s=2 * W, v_s=2 * W)
    for name, columns in (whole_rows | half_rows).items():
        height = share // 2 if name in half_rows else share
        scratch["p_" + name] = vmem(n, height, columns)
        scratch["l_" + name] = vmem(n, height, columns)
    sems("gather", 7, n)
    sems("reduce", len(whole_rows) + len(half_rows), n)
    sems("spread", 7, 3 * LOTS)
    sems("collect", 7, 2 + LOTS)
    sems("small", steps)
    names = list(operands) + list(outs) + list(scratch)
    results = pl.pallas_call(
        lambda *refs: layer_kernel(names, inner, *refs),
        out_shape=tuple(outs.values()),
        in_specs=[pl.BlockSpec(memory_space=pltpu.VMEM)] * len(operands),
        out_specs=tuple(pl.BlockSpec(memory_space=pltpu.VMEM) for _ in outs),
        scratch_shapes=list(scratch.values()),
        name="layer",
        compiler_params=pltpu.CompilerParams(
            collective_id=1, has_side_effects=True, vmem_limit_bytes=VMEM_LIMIT
        ),
    )(*operands.values())
    return dict(zip(outs, results, strict=True))


def write_kernel(names, *refs):
    r = Names(names, refs)
    W = r.o_wo_s.shape[1]
    D = r.layer_out.shape[1]
    own = r.grad_scales.shape[1]
    r.layer[...] = r.layer_out[...]
    r.back[...] = r.grad_in[...]
    r.encoder[...] = r.grad_source[...]
    r.wq_s[...] = r.o_qk_s[:, :W]
    r.wk_s[...] = r.o_qk_s[:, W:]
    r.wv_s[...] = r.o_v_s[...]
    r.wo_s[...] = jnp.transpose(r.o_wo_s[...])
    r.wq_c[...] = r.o_qo_c[:, :W]
    r.wk_c[...] = r.o_kv_c[:, :W]
    r.wv_c[...] = r.o_kv_c[:, W:]
    r.wo_c[...] = jnp.transpose(r.o_qo_c[:, W:])
    r.w_gate[...] = r.o_gate[...]
    r.w_up[...] = r.o_up[...]
    r.w_down[...] = r.o_dn[...]
    place = lax.axis_index("dp") * lax.axis_size("tensor") + lax.axis_index("tensor")
    turn = lax.rem(D - place * own, D)
    r.grad_scales[...] = pltpu.roll(r.small_out[1], turn, 1)[:3, :own]
    sums = jnp.concatenate(
        [
            jnp.sum(r.indicator[...] * r.small_out[0][3 + h:4 + h, :L], axis=1, keepdims=True)
            for h in range(W // DH)
        ],
        axis=1,
    )
    r.grad_bias[...] = jnp.transpose(sums)


def write_out(sums, indicator):
    rows, D = sums["layer_out"].shape
    share, W = sums["o_wo_s"].shape
    F = sums["o_dn"].shape[1]
    devices = lax.axis_size("dp") * lax.axis_size("tensor")
    square = whole((share, W), F32)
    turned = whole((W, share), F32)
    wide = whole((share, F), F32)
    outs = dict(
        layer=whole((rows, D), BF16),
        back=whole((rows, D), F32),
        encoder=whole((rows, D), F32),
        wq_s=square,
        wk_s=square,
        wv_s=square,
        wo_s=turned,
        wq_c=square,
        wk_c=square,
        wv_c=square,
        wo_c=turned,
        w_gate=wide,
        w_up=wide,
        w_down=wide,
        grad_scales=whole((3, D // devices), F32),
        grad_bias=whole((W // DH, NBUCKET), F32),
    )
    operands = dict(sums, indicator=indicator)
    names = list(operands) + list(outs)
    results = pl.pallas_call(
        lambda *refs: write_kernel(names, *refs),
        out_shape=tuple(outs.values()),
        in_specs=[pl.BlockSpec(memory_space=pltpu.VMEM)] * len(operands),
        out_specs=tuple(pl.BlockSpec(memory_space=pltpu.VMEM) for _ in outs),
        name="write_out",
        compiler_params=pltpu.CompilerParams(vmem_limit_bytes=VMEM_LIMIT),
    )(*operands.values())
    final = dict(zip(outs, results, strict=True))
    final.update(w_down=final["w_down"].T, grad_bias=final["grad_bias"].T)
    return tuple(final.values())


def per_device(
    layer_in,
    encoder_states,
    grad_out,
    buckets,
    keep,
    wq_self,
    wk_self,
    wv_self,
    wo_self,
    wq_cross,
    wk_cross,
    wv_cross,
    wo_cross,
    w_gate,
    w_up,
    w_down,
    norm_scales,
    rel_bias,
):
    size = lax.axis_size("dp")
    inner = 1
    while (wq_self.shape[0] * inner) % (2 * ROW_TILE) and inner < size:
        inner *= 2
    groups = [list(range(start, start + inner)) for start in range(0, size, inner)]

    def joined(weights, axis):
        if inner == 1:
            return weights
        return lax.all_gather(weights, "dp", axis=axis, tiled=True, axis_index_groups=groups)

    indicator = jnp.asarray(distance_indicator())
    operands = dict(
        layer_in=layer_in,
        source=encoder_states,
        grad_out=grad_out,
        keep=keep,
        wq_s=joined(wq_self, 0),
        wk_s=joined(wk_self, 0),
        wv_s=joined(wv_self, 0),
        wo_s=joined(wo_self, 1),
        wq_c=joined(wq_cross, 0),
        wk_c=joined(wk_cross, 0),
        wv_c=joined(wv_cross, 0),
        wo_c=joined(wo_cross, 1),
        w_gate=joined(w_gate, 0),
        w_up=joined(w_up, 0),
        w_down=joined(w_down, 1).T,
        scales=joined(norm_scales, 1),
        rel_bias=rel_bias.T,
        indicator=indicator,
    )
    sums = run_layer(inner, operands)
    if inner > 1:
        for name in [name for name in sums if name.startswith("o_")]:
            sums[name] = lax.psum_scatter(
                sums[name], "dp", scatter_dimension=0, tiled=True, axis_index_groups=groups
            )
    return write_out(sums, indicator)


def solution(mesh):
    in_specs = (
        P(("dp", "tensor"), None),
        P(("dp", "tensor"), None),
        P(("dp", "tensor"), None),
        P("dp", None, None),
        P("dp", None, None),
        P("dp", "tensor"),
        P("dp", "tensor"),
        P("dp", "tensor"),
        P("tensor", "dp"),
        P("dp", "tensor"),
        P("dp", "tensor"),
        P("dp", "tensor"),
        P("tensor", "dp"),
        P("dp", "tensor"),
        P("dp", "tensor"),
        P("tensor", "dp"),
        P(None, "dp"),
        P(None, "tensor"),
    )
    out_specs = (
        P(("dp", "tensor"), None),
        P(("dp", "tensor"), None),
        P(("dp", "tensor"), None),
        P("dp", "tensor"),
        P("dp", "tensor"),
        P("dp", "tensor"),
        P("tensor", "dp"),
        P("dp", "tensor"),
        P("dp", "tensor"),
        P("dp", "tensor"),
        P("tensor", "dp"),
        P("dp", "tensor"),
        P("dp", "tensor"),
        P("tensor", "dp"),
        P(None, ("dp", "tensor")),
        P(None, "tensor"),
    )
    return jax.shard_map(
        per_device, mesh=mesh, in_specs=in_specs, out_specs=out_specs, check_vma=False
    )
```
